512 devices in a mesh: seq: 64 (over z, y), ch: 8 (over x, core).
Axes of the slice: x: 4, y: 4, z: 16, core: 2. Of those that a mesh axis runs over, the one named last changes fastest.
Arguments:
- normalized_layer_entry: bfloat16 [8192, 4096], P('seq', 'ch'), may hold values from -6 to 6
- short_outer_query: bfloat16 [8192, 4096], P('seq', 'ch'), may hold values from -6 to 6
- short_inner_key: bfloat16 [8192, 4096], P('seq', 'ch'), may hold values from -6 to 6
- short_frozen_value: bfloat16 [8192, 4096], P('seq', 'ch'), may hold values from -6 to 6
- medium_outer_query: bfloat16 [8192, 4096], P('seq', 'ch'), may hold values from -6 to 6
- medium_inner_key: bfloat16 [8192, 4096], P('seq', 'ch'), may hold values from -6 to 6
- cotangent: bfloat16 [8192, 4096], P('seq', 'ch'), may hold values from -6 to 6
- adapter_down_factor: bfloat16 [64, 32, 4096], P('seq', None, 'ch'), may hold values from -0.09375 to 0.09375
- adapter_up_factor: bfloat16 [64, 32, 4096], P('seq', None, 'ch'), may hold values from -1 to 1
- token_clade: int32 [8192, 1], P('seq'), may hold values from 0 to 63; in each aligned block of 128 rows (0 to 127, 128 to 255, ...) at most 4 rows name the same one
- clade_storage_slot: int32 [64], replicated, may hold values from 0 to 63, each once
- short_group_filter: float32 [256, 7], P('ch'), may hold values from -2.4 to 2.4
- medium_undamped_filter: float32 [256, 128], P('ch'), may hold values from -0.6 to 0.6
- medium_decay_rate: float32 [256], P('ch'), may hold values from 0.003 to 0.06
Outputs:
- midrange_response: bfloat16 [8192, 4096], P('seq', 'ch')
- layer_entry_derivative: bfloat16 [8192, 4096], P('seq', 'ch')
- lowdim_projector_derivative: float32 [64, 32, 4096], P('seq', None, 'ch')
- lowdim_expander_derivative: float32 [64, 32, 4096], P('seq', None, 'ch')
- brief_convolution_derivative: float32 [256, 7], P('ch')
- midrange_raw_response_derivative: float32 [256, 128], P('ch')
The draws below stay inside these ranges and needn't reach their ends.
Inputs may be any that keep to these rules, and one draw needn't show every extreme that they name: `token_clade`: among the 128 tokens of one device, no clade is named more than 4 times, a bound that some block reaches. `clade_storage_slot`: each slot holds exactly one clade's adapter.
All inputs are finite; a program needn't handle non-finite values.
Results may differ from the reference program's by a relative error of at most 0.012.
Values may be sent and summed in bfloat16 or wider, within the bound.
A program may use at most 64 MiB of HBM per device.

```python
import math
import jax
import jax.numpy as jnp
import numpy as np
from jax import lax

MODEL_WIDTH = 4096
GS = 16
LSE = 7
MEDIUM_TAPS_LEN = 128
ADAPTER_RANK = 32
TOKENS_PER_SHARD = 128
TOKENS = 8192
ADAPTED_CLADES = 64
CAP = 4
FILTER_GROUPS = 256
N_SEQ = 64


def block_levels(own_key, extent, shards, low, top_value):
    gain, own = 1.0, jax.random.fold_in(own_key, 6)
    for axis_at, parts in shards:
        steps = jnp.exp(jax.random.uniform(jax.random.fold_in(own, axis_at), (parts,), jnp.float32, low / len(shards), top_value / len(shards)))
        gain = gain * jnp.repeat(steps, extent[axis_at] // parts).reshape([-1 if axis == axis_at else 1 for axis in range(len(extent))])
    return gain


def assign_block(own_key, own, number, rows, amount, top, most, lean):
    order = jax.random.permutation(own_key, amount)
    heavy_load, usual = load_shares(amount, rows * top, most, lean, True), load_shares(amount, rows * top, most, lean, False)
    places = jnp.arange(amount)

    def named(lengths, turn):
        used = int((lengths > 0).sum())
        fixed = max(1, used // 4)
        shifted = fixed + (places - fixed + turn * (used - fixed)) % max(1, amount - fixed)
        return jnp.zeros((amount,), jnp.int32).at[order[jnp.where(places < fixed, places, shifted)]].set(jnp.asarray(lengths, jnp.int32))

    lengths = jnp.where(number % 4 == 0, named(heavy_load, number // 4), named(usual, number - number // 4 - 1))
    mixed = jax.random.permutation(jax.random.fold_in(own, 3), amount)
    giver, receiver = mixed[0:amount // 2 * 2:2], mixed[1:amount // 2 * 2:2]
    margin = jnp.minimum(lengths[giver] - 1, most - lengths[receiver]) // 2
    margin = jnp.where((giver == order[0]) | (receiver == order[0]) | (lengths[receiver] == 0), 0, jnp.maximum(margin, 0))
    shifted = jax.random.randint(jax.random.fold_in(own, 4), (amount // 2,), 0, 1 << 20) % (margin + 1)
    lengths = lengths.at[giver].add(-shifted).at[receiver].add(shifted)
    items = jnp.searchsorted(jnp.cumsum(lengths), jnp.arange(rows * top), side="right").astype(jnp.int32)
    listing = items.reshape(top, rows).T
    listing = listing[jax.random.permutation(jax.random.fold_in(own, 1), rows)]
    turn = jax.random.randint(jax.random.fold_in(own, 2), (rows, 1), 0, top)
    return jnp.take_along_axis(listing, (jnp.arange(top)[None, :] + turn) % top, axis=1)


def load_shares(count, total, bound, slope, full):
    portions = [(1 << 20) // math.isqrt(grade ** slope) + 1 for grade in range(1, count + 1)]
    largest = bound if full else min(bound, max(-(-total // count), total * portions[0] // sum(portions)))
    least = 1 if total - largest >= count - 1 else 0
    given, spare = [largest] + [least] * (count - 1), total - largest - least * (count - 1)
    while spare > 0:
        movable = [i for i in range(1, count) if given[i] < largest] or [i for i in range(1, count) if given[i] < bound]
        mass, left = sum([portions[i] for i in movable]), spare
        for i in movable:
            extra = min(bound - given[i], max(1, left * portions[i] // mass), spare)
            given[i] = given[i] + extra
            spare = spare - extra
    return np.array(given)


def gaussian(stream_key, shape, deviation, limit, split=(), kind=jnp.bfloat16):
    values = deviation * jax.random.normal(stream_key, shape, jnp.float32)
    if split:
        values = values * block_levels(stream_key, shape, split, -0.22, 0.18)
    return jnp.clip(values, -limit, limit).astype(kind)


def setup_inputs(seed: int = 0) -> dict:
    streams_of = jax.random.split(jax.random.key(seed), 15)
    normalized_layer_entry = gaussian(streams_of[0], (TOKENS, MODEL_WIDTH), 1.0, 6.0, ((0, 64), (1, 8)))
    short_outer_query = gaussian(streams_of[1], (TOKENS, MODEL_WIDTH), 1.0, 6.0, ((0, 64), (1, 8)))
    short_inner_key = gaussian(streams_of[2], (TOKENS, MODEL_WIDTH), 1.0, 6.0, ((0, 64), (1, 8)))
    short_frozen_value = gaussian(streams_of[3], (TOKENS, MODEL_WIDTH), 1.0, 6.0, ((0, 64), (1, 8)))
    medium_outer_query = gaussian(streams_of[4], (TOKENS, MODEL_WIDTH), 1.0, 6.0, ((0, 64), (1, 8)))
    medium_inner_key = gaussian(streams_of[5], (TOKENS, MODEL_WIDTH), 1.0, 6.0, ((0, 64), (1, 8)))
    cotangent = gaussian(streams_of[6], (TOKENS, MODEL_WIDTH), 1.0, 6.0, ((0, 64), (1, 8)))
    adapter_down_factor = gaussian(streams_of[7], (ADAPTED_CLADES, ADAPTER_RANK, MODEL_WIDTH), MODEL_WIDTH ** -0.5, 0.09375, ((0, 64), (2, 8)))
    adapter_up_factor = gaussian(streams_of[8], (ADAPTED_CLADES, ADAPTER_RANK, MODEL_WIDTH), ADAPTER_RANK ** -0.5, 1.0, ((0, 64), (2, 8)))
    token_clade_keys = jax.random.split(jax.random.fold_in(streams_of[9], 1), TOKENS // TOKENS_PER_SHARD)
    token_clade_turns = jax.random.permutation(jax.random.fold_in(streams_of[9], 3), TOKENS // TOKENS_PER_SHARD)
    token_clade = jax.vmap(lambda own, number: assign_block(jax.random.fold_in(streams_of[9], 2), own, number, TOKENS_PER_SHARD, ADAPTED_CLADES, 1, CAP, 2))(token_clade_keys, token_clade_turns).reshape((TOKENS, 1))
    clade_storage_slot = jax.random.permutation(streams_of[10], ADAPTED_CLADES).astype(jnp.int32)
    short_group_filter = gaussian(streams_of[11], (FILTER_GROUPS, LSE), 0.4, 2.4, ((0, 8),), jnp.float32)
    medium_undamped_filter = gaussian(streams_of[12], (FILTER_GROUPS, MEDIUM_TAPS_LEN), 0.1, 0.6, ((0, 8),), jnp.float32)
    medium_decay_rate = jnp.clip(jnp.exp(math.log(0.06) - 2.9957322 * jax.random.uniform(streams_of[13], (FILTER_GROUPS,), jnp.float32) ** block_levels(streams_of[13], (FILTER_GROUPS,), ((0, 8),), -0.2, 0.2)), 0.003, 0.06)
    return dict(normalized_layer_entry=normalized_layer_entry, short_outer_query=short_outer_query, short_inner_key=short_inner_key, short_frozen_value=short_frozen_value, medium_outer_query=medium_outer_query, medium_inner_key=medium_inner_key, cotangent=cotangent, adapter_down_factor=adapter_down_factor, adapter_up_factor=adapter_up_factor, token_clade=token_clade, clade_storage_slot=clade_storage_slot, short_group_filter=short_group_filter, medium_undamped_filter=medium_undamped_filter, medium_decay_rate=medium_decay_rate)


def causal_conv(values, kernel):
    taps = kernel.shape[1]
    sequence_length = values.shape[0]
    padded = jnp.pad(values, ((taps - 1, 0), (0, 0)))

    def add_tap(index, total):
        start = (taps - 1 - index).astype(jnp.int32)
        piece = lax.dynamic_slice_in_dim(padded, start, sequence_length, 0)
        return total + piece * lax.dynamic_index_in_dim(kernel, index, 1, keepdims=False)[None, :]
    return lax.fori_loop(jnp.int32(0), jnp.int32(taps), add_tap, jnp.zeros(values.shape, jnp.float32))

def anti_conv(values, kernel):
    taps = kernel.shape[1]
    sequence_length = values.shape[0]
    padded = jnp.pad(values, ((0, taps - 1), (0, 0)))

    def add_tap(index, total):
        start = index.astype(jnp.int32)
        piece = lax.dynamic_slice_in_dim(padded, start, sequence_length, 0)
        return total + piece * lax.dynamic_index_in_dim(kernel, index, 1, keepdims=False)[None, :]
    return lax.fori_loop(jnp.int32(0), jnp.int32(taps), add_tap, jnp.zeros(values.shape, jnp.float32))

def kernel_gradient(grad_out, values, taps):
    sequence_length = values.shape[0]
    padded = jnp.pad(values, ((taps - 1, 0), (0, 0)))

    def one_tap(index):
        start = (taps - 1 - index).astype(jnp.int32)
        piece = lax.dynamic_slice_in_dim(padded, start, sequence_length, 0)
        return lax.optimization_barrier(jnp.sum(grad_out * piece, axis=0))
    per_channel = lax.map(one_tap, jnp.arange(taps, dtype=jnp.int32)).T
    return per_channel.reshape(FILTER_GROUPS, GS, taps).sum(axis=1)

def token_totals(first, slots, table, form):
    block = math.gcd(TOKENS, 256)
    count = TOKENS // block

    def one_block(pair):
        inputs, owners = pair
        return jnp.einsum(form, inputs.astype(jnp.float32), table[owners].astype(jnp.float32), precision=lax.Precision.HIGHEST)
    result = lax.map(one_block, (first.reshape(count, block, first.shape[1]), slots.reshape(count, block)))
    return result.reshape(TOKENS, result.shape[-1])

def bucket_counts(slots, left, right):
    most = N_SEQ * CAP
    order = jnp.argsort(slots, stable=True)
    sorted_slot = jnp.concatenate([slots[order], jnp.full((most,), -1, jnp.int32)])
    sorted_left = jnp.concatenate([left[order], jnp.zeros((most, left.shape[1]), left.dtype)])
    sorted_right = jnp.concatenate([right[order], jnp.zeros((most, right.shape[1]), right.dtype)])
    counts = lax.optimization_barrier(jnp.sum((slots[:, None] == jnp.arange(ADAPTED_CLADES, dtype=jnp.int32)[None, :]).astype(jnp.int32), axis=0))
    starts = (jnp.cumsum(counts) - counts).astype(jnp.int32)

    def one_slot(index):
        start = starts[index].astype(jnp.int32)
        keep = (lax.dynamic_slice_in_dim(sorted_slot, start, most, 0) == index)[:, None]
        part_left = jnp.where(keep, lax.dynamic_slice_in_dim(sorted_left, start, most, 0), jnp.zeros((), left.dtype))
        part_right = lax.dynamic_slice_in_dim(sorted_right, start, most, 0)
        return jnp.dot(part_left.T, part_right, preferred_element_type=jnp.float32)
    return lax.map(one_slot, jnp.arange(ADAPTED_CLADES, dtype=jnp.int32))

def reference(normalized_layer_entry, short_outer_query, short_inner_key, short_frozen_value, medium_outer_query, medium_inner_key, cotangent, adapter_down_factor, adapter_up_factor, token_clade, clade_storage_slot, short_group_filter, medium_undamped_filter, medium_decay_rate):
    memory_bucket = clade_storage_slot[token_clade[:, 0]].astype(jnp.int32)
    lineage_labels = token_totals(normalized_layer_entry, memory_bucket, adapter_down_factor, 'gi,gbi->gb').astype(jnp.bfloat16)
    adapter_update = (0.5 * token_totals(lineage_labels, memory_bucket, adapter_up_factor, 'np,npz->nz')).astype(jnp.bfloat16)
    short_in = (short_inner_key.astype(jnp.float32) * (short_frozen_value.astype(jnp.float32) + adapter_update.astype(jnp.float32))).astype(jnp.bfloat16)
    short_channel = jnp.repeat(short_group_filter, GS, axis=0)
    short_conv = causal_conv(short_in.astype(jnp.float32), short_channel)
    medium_operator_input = (medium_inner_key.astype(jnp.float32) * short_outer_query.astype(jnp.float32) * short_conv).astype(jnp.bfloat16)
    decay_envelope = jnp.exp(-medium_decay_rate[:, None] * jnp.arange(MEDIUM_TAPS_LEN, dtype=jnp.float32)[None, :])
    medium_taps = medium_undamped_filter * decay_envelope
    medium_channel = jnp.repeat(medium_taps, GS, axis=0)
    medium_conv = causal_conv(medium_operator_input.astype(jnp.float32), medium_channel)
    midrange_response = (medium_outer_query.astype(jnp.float32) * medium_conv).astype(jnp.bfloat16)
    filter_gradient_scale = 1.0 / math.sqrt(TOKENS * GS)
    medium_gradient = (cotangent.astype(jnp.float32) * medium_outer_query.astype(jnp.float32)).astype(jnp.bfloat16)
    medium_in_grad = anti_conv(medium_gradient.astype(jnp.float32), medium_channel)
    midrange_raw_response_derivative = kernel_gradient(medium_gradient.astype(jnp.float32), medium_operator_input.astype(jnp.float32), MEDIUM_TAPS_LEN) * decay_envelope * filter_gradient_scale
    short_grad = (medium_in_grad * medium_inner_key.astype(jnp.float32) * short_outer_query.astype(jnp.float32)).astype(jnp.bfloat16)
    short_in_grad = anti_conv(short_grad.astype(jnp.float32), short_channel)
    brief_convolution_derivative = kernel_gradient(short_grad.astype(jnp.float32), short_in.astype(jnp.float32), LSE) * filter_gradient_scale
    correction_delta_derivative = (0.5 * short_in_grad * short_inner_key.astype(jnp.float32)).astype(jnp.bfloat16)
    lineage_labels_derivative = token_totals(correction_delta_derivative, memory_bucket, adapter_up_factor, 'gi,gbi->gb').astype(jnp.bfloat16)
    layer_entry_derivative = token_totals(lineage_labels_derivative, memory_bucket, adapter_down_factor, 'np,npz->nz').astype(jnp.bfloat16)
    correction_multiplier = 1.0 / math.sqrt(TOKENS_PER_SHARD)
    lowdim_expander_derivative = bucket_counts(memory_bucket, lineage_labels, correction_delta_derivative) * correction_multiplier
    lowdim_projector_derivative = bucket_counts(memory_bucket, lineage_labels_derivative, normalized_layer_entry) * correction_multiplier
    return (midrange_response, layer_entry_derivative, lowdim_projector_derivative, lowdim_expander_derivative, brief_convolution_derivative, midrange_raw_response_derivative)
```

```python
import functools
import math

import jax
import jax.numpy as jnp
from jax import lax
from jax.experimental import pallas as pl
from jax.experimental.pallas import tpu as pltpu
from jax.sharding import PartitionSpec as P

F32, BF16 = jnp.float32, jnp.bfloat16
MESH = pl.DeviceIdType.MESH
LANES = 128
(MG_HALO, SG_HALO, SI_HALO, MED_HALO, X_OUT, DG_OUT, DELTA_BACK, DX_BACK, CODES, CODES_GRAD, SUM_Y, SUM_Z, SPREAD_Y) = range(13)


def mm(left, right):
    return jnp.dot(left, right, preferred_element_type=F32)


def mm_t(left, right, precision=None):
    return lax.dot_general(
        left, right, (((1,), (1,)), ((), ())), precision=precision, preferred_element_type=F32
    )


def t_mm(left, right, precision=None):
    return lax.dot_general(
        left, right, (((0,), (0,)), ((), ())), precision=precision, preferred_element_type=F32
    )


def iota(shape, axis):
    return lax.broadcasted_iota(jnp.int32, shape, axis)


def lane_block(index):
    return pl.ds(pl.multiple_of(index * LANES, LANES), LANES)


def stacked(value):
    return jnp.concatenate(
        [value[:, b * LANES : (b + 1) * LANES] for b in range(value.shape[1] // LANES)], axis=0
    )


def kernel(
    n_seq, n_ch, n_y, cap,
    x, soq, sik, sfv, moq, mik, cot, down, up, clade, storage, short_filter, medium_filter, rate,
    response, dx_out, projector, expander, brief, midrange,
    place, place_t, swap, toep_b, toep_f, mgext, sgext, siext, medext,
    xs, xr, ds, dr, us, ur, es, er, yx, yd, codes_all, cgrad_all, fg, yr, zr, fr, taps, mirror,
    send, recv,
):
    tokens, width = x.shape
    blocks = width // LANES
    slots = n_seq * cap
    chunk = blocks * cap
    groups = short_filter.shape[0]
    short_len = short_filter.shape[1]
    per_block = groups // blocks
    size = width // groups
    n_z = n_seq // n_y
    me, mine = lax.axis_index("seq"), lax.axis_index("ch")
    my_z, my_y = me // n_y, lax.rem(me, n_y)

    def push(kind, source, target, device):
        pltpu.make_async_remote_copy(
            src_ref=source, dst_ref=target, send_sem=send.at[kind], recv_sem=recv.at[kind],
            device_id=device, device_id_type=MESH,
        ).start()

    def landed(kind, ref):
        pltpu.make_async_copy(ref, ref, recv.at[kind]).wait()

    def gone(kind, ref):
        pltpu.make_async_copy(ref, ref, send.at[kind]).wait()

    def rows_of(ref, device):
        return ref.at[pl.ds(pl.multiple_of(device * chunk, chunk), chunk), :]

    def exchange(kind, source, target):
        @pl.loop(1, n_seq)
        def _(step):
            peer = lax.rem(me + step, n_seq)
            push(kind, rows_of(source, peer), rows_of(target, me), {"seq": peer})

        pltpu.make_async_copy(rows_of(source, me), rows_of(target, me), recv.at[kind]).start()

    def share(kind, ref):
        @pl.loop(1, n_ch)
        def _(step):
            peer = lax.rem(mine + step, n_ch)
            push(kind, ref.at[mine], ref.at[mine], {"ch": peer})

    barrier = pltpu.get_barrier_semaphore()

    @pl.loop(1, n_seq)
    def _(step):
        pl.semaphore_signal(
            barrier, inc=1, device_id={"seq": lax.rem(me + step, n_seq)}, device_id_type=MESH
        )

    @pl.loop(1, n_ch)
    def _(step):
        pl.semaphore_signal(
            barrier, inc=1, device_id={"ch": lax.rem(mine + step, n_ch)}, device_id_type=MESH
        )

    square = (tokens, tokens)
    eye = iota(square, 0) == iota(square, 1)
    clade_row = jnp.sum(jnp.where(eye, clade[...], 0).astype(F32), axis=0, keepdims=True)
    clade_col = clade[...].astype(F32)
    earlier = (clade_col == clade_row) & (iota(square, 1) < iota(square, 0))
    rank = jnp.sum(jnp.where(earlier, 1.0, 0.0), axis=1, keepdims=True)
    names = iota((tokens, n_seq), 1).astype(F32)
    owner = jnp.sum(
        jnp.where(clade_col == names, storage[...].astype(F32), 0.0), axis=1, keepdims=True
    )
    key_col = owner * chunk + rank
    key_row = jnp.sum(jnp.where(eye, key_col, 0.0), axis=0, keepdims=True).astype(jnp.int32)
    key_col = key_col.astype(jnp.int32)
    for b in range(blocks):
        lanes = slice(b * LANES, (b + 1) * LANES)
        place[:, lanes] = jnp.where(
            iota((slots * blocks, tokens), 0) == key_row + b * cap, 1.0, 0.0
        ).astype(BF16)
    xs[...] = mm(place[...], stacked(x[...])).astype(BF16)
    mgext[0:tokens, :] = (cot[...].astype(F32) * moq[...].astype(F32)).astype(BF16)

    pl.semaphore_wait(barrier, n_seq - 1 + n_ch - 1)

    @pl.when(me > 0)
    def _():
        push(MG_HALO, mgext.at[0:tokens, :], mgext.at[tokens : 2 * tokens, :], {"seq": me - 1})

    exchange(X_OUT, xs, xr)

    eye_g = iota((groups, groups), 0) == iota((groups, groups), 1)
    rate_col = jnp.sum(jnp.where(eye_g, rate[...], 0.0), axis=1, keepdims=True)
    envelope = jnp.exp(-rate_col * iota((groups, LANES), 1).astype(F32))
    damped = medium_filter[...] * envelope
    turned = jnp.where(
        iota(square, 0) == lax.rem(tokens - iota(square, 1), tokens), 1.0, 0.0
    ).astype(BF16)
    taps[...] = damped
    mirror[...] = mm(damped.astype(BF16), turned)
    row, col = iota(square, 0), iota(square, 1)

    @pl.loop(0, groups)
    def _(g):
        for source, target, own in ((taps, toep_b, col >= row), (mirror, toep_f, col <= row)):
            wide = jnp.broadcast_to(source[pl.ds(g, 1), :], square)
            band = pltpu.roll(wide, 0, 1, stride=1, stride_axis=0)
            target[g, :, 0:tokens] = jnp.where(own, band, 0.0).astype(BF16)
            target[g, :, tokens : 2 * tokens] = jnp.where(own, 0.0, band).astype(BF16)

    of_group = jnp.where(
        iota((groups, width), 1) // size == iota((groups, width), 0), 1.0, 0.0
    )
    short_wide = t_mm(short_filter[...], of_group, lax.Precision.HIGHEST)
    lane_group = iota(square, 1) // size

    def banded(ref, bands, b):
        data = ref[:, lane_block(b)]
        total = jnp.zeros(square, F32)
        for q in range(per_block):
            total = jnp.where(lane_group == q, mm(bands[b * per_block + q], data), total)
        return total

    @pl.when(me < n_seq - 1)
    def _():
        landed(MG_HALO, mgext.at[tokens : 2 * tokens, :])

    @pl.when(me == n_seq - 1)
    def _():
        mgext[tokens : 2 * tokens, :] = jnp.zeros((tokens, width), BF16)

    @pl.loop(0, blocks)
    def _(b):
        lanes = lane_block(b)
        gates = mik[:, lanes].astype(F32) * soq[:, lanes].astype(F32)
        sgext[0:tokens, lanes] = (banded(mgext, toep_b, b) * gates).astype(BF16)

    @pl.when(me > 0)
    def _():
        push(SG_HALO, sgext.at[0:16, :], sgext.at[tokens : tokens + 16, :], {"seq": me - 1})

    part = 2 * LANES
    per_part = part // blocks
    at = iota((part, part), 0)
    inside = lax.rem(at, per_part)
    wanted = (inside // cap) * chunk + (at // per_part) * cap + lax.rem(inside, cap)
    swap[...] = jnp.where(iota((part, part), 1) == wanted, 1.0, 0.0).astype(BF16)

    def opened(packed, target):
        for p in range(slots // per_part):
            turned_rows = mm(swap[...], packed[p * part : (p + 1) * part, :]).astype(BF16)
            for b in range(blocks):
                target[p * per_part : (p + 1) * per_part, b * LANES : (b + 1) * LANES] = (
                    turned_rows[b * per_part : (b + 1) * per_part]
                )

    def closed(value, packed):
        for p in range(slots // per_part):
            piece = stacked(value[p * per_part : (p + 1) * per_part])
            packed[p * part : (p + 1) * part, :] = t_mm(swap[...], piece).astype(BF16)

    landed(X_OUT, xr)
    opened(xr, yx)
    codes_all[mine] = mm_t(down[0], yx[...])
    share(CODES, codes_all)

    @pl.when(me < n_seq - 1)
    def _():
        landed(SG_HALO, sgext.at[tokens : tokens + 16, :])

    @pl.when(me == n_seq - 1)
    def _():
        sgext[tokens : tokens + 16, :] = jnp.zeros((16, width), BF16)

    ahead = sgext[...].astype(F32)
    total = jnp.zeros((tokens, width), F32)
    for j in range(short_len):
        total = total + short_wide[j : j + 1, :] * ahead[j : j + tokens]
    delta_grad = (0.5 * total * sik[...].astype(F32)).astype(BF16)
    ds[...] = mm(place[...], stacked(delta_grad)).astype(BF16)
    exchange(DG_OUT, ds, dr)

    def summed(ref):
        total = ref[0]
        for c in range(1, ref.shape[0]):
            total = total + ref[c]
        return total

    landed(CODES, codes_all.at[0 : n_ch - 1])
    codes = summed(codes_all).astype(BF16)
    closed((0.5 * t_mm(codes, up[0])).astype(BF16), us)
    exchange(DELTA_BACK, us, ur)

    for b in range(blocks):
        place_t[b * tokens : (b + 1) * tokens, :] = jnp.where(
            iota((tokens, slots * blocks), 1) == key_col + b * cap, 1.0, 0.0
        ).astype(BF16)

    weight_scale = 1.0 / math.sqrt(tokens)
    landed(DG_OUT, dr)
    opened(dr, yd)
    cgrad_all[mine] = mm_t(up[0], yd[...])
    share(CODES_GRAD, cgrad_all)
    expander[0] = mm(codes, yd[...]) * weight_scale

    landed(DELTA_BACK, ur)
    delta = mm(place_t[...], ur[...]).astype(BF16).astype(F32)
    for b in range(blocks):
        lanes = slice(b * LANES, (b + 1) * LANES)
        siext[16 : 16 + tokens, lanes] = (
            sik[:, lanes].astype(F32)
            * (sfv[:, lanes].astype(F32) + delta[b * tokens : (b + 1) * tokens])
        ).astype(BF16)

    @pl.when(me < n_seq - 1)
    def _():
        push(SI_HALO, siext.at[tokens : tokens + 16, :], siext.at[0:16, :], {"seq": me + 1})

    landed(CODES_GRAD, cgrad_all.at[0 : n_ch - 1])
    codes_grad = summed(cgrad_all).astype(BF16)
    closed(t_mm(codes_grad, down[0]).astype(BF16), es)
    exchange(DX_BACK, es, er)

    @pl.when(me > 0)
    def _():
        landed(SI_HALO, siext.at[0:16, :])

    @pl.when(me == 0)
    def _():
        siext[0:16, :] = jnp.zeros((16, width), BF16)

    behind = siext[...].astype(F32)
    total = jnp.zeros((tokens, width), F32)
    for j in range(short_len):
        total = total + short_wide[j : j + 1, :] * behind[16 - j : 16 - j + tokens]
    medext[0:tokens, :] = (mik[...].astype(F32) * soq[...].astype(F32) * total).astype(BF16)

    @pl.when(me < n_seq - 1)
    def _():
        push(MED_HALO, medext.at[0:tokens, :], medext.at[tokens : 2 * tokens, :], {"seq": me + 1})

    projector[0] = mm(codes_grad, yx[...]) * weight_scale
    short_grad = sgext[0:tokens, :].astype(F32)
    fg[:, 8:16, :] = jnp.zeros((blocks, 8, LANES), F32)
    for j in range(short_len):
        line = jnp.sum(short_grad * behind[16 - j : 16 - j + tokens], axis=0, keepdims=True)
        for b in range(blocks):
            fg[b, 8 + j : 9 + j, :] = line[:, b * LANES : (b + 1) * LANES]

    @pl.when(me > 0)
    def _():
        landed(MED_HALO, medext.at[tokens : 2 * tokens, :])

    @pl.when(me == 0)
    def _():
        medext[tokens : 2 * tokens, :] = jnp.zeros((tokens, width), BF16)

    flip = jnp.where(row + col == tokens - 1, 1.0, 0.0).astype(BF16)

    @pl.loop(0, blocks)
    def _(b):
        lanes = lane_block(b)
        grads = mgext[0:tokens, lanes].astype(F32)
        data = jnp.concatenate(
            [
                mm(flip, medext[0:tokens, lanes]).astype(BF16),
                mm(flip, medext[tokens : 2 * tokens, lanes]).astype(BF16),
            ],
            axis=0,
        )
        for q in range(per_block):
            masked = jnp.where(lane_group == q, grads, 0.0).astype(BF16)
            product = mm_t(masked, data)
            merged = jnp.where(
                col + row >= tokens - 1, product[:, 0:tokens], product[:, tokens : 2 * tokens]
            )
            lined = pltpu.roll(merged, 1, 1, stride=1, stride_axis=0)
            fg[b, q : q + 1, :] = jnp.sum(lined, axis=0, keepdims=True)

    yr[my_y] = fg[my_y]

    @pl.loop(1, n_y)
    def _(step):
        peer = lax.rem(my_y + step, n_y)
        push(SUM_Y, fg.at[peer], yr.at[my_y], {"seq": my_z * n_y + peer})

    def respond(b):
        lanes = lane_block(b)
        response[:, lanes] = (
            banded(medext, toep_f, b) * moq[:, lanes].astype(F32)
        ).astype(BF16)

    @pl.loop(0, blocks // 2)
    def _(b):
        respond(b)

    landed(SUM_Y, yr.at[0 : n_y - 1])
    zr[my_z] = summed(yr)

    @pl.loop(1, n_z)
    def _(step):
        peer = lax.rem(my_z + step, n_z)
        push(SUM_Z, zr.at[my_z], zr.at[my_z], {"seq": peer * n_y + my_y})

    @pl.loop(blocks // 2, blocks)
    def _(b):
        respond(b)

    landed(DX_BACK, er)
    back = mm(place_t[...], er[...]).astype(BF16)
    for b in range(blocks):
        dx_out[:, b * LANES : (b + 1) * LANES] = back[b * tokens : (b + 1) * tokens]

    landed(SUM_Z, zr.at[0 : n_z - 1])
    fr[my_y] = summed(zr)

    @pl.loop(1, n_y)
    def _(step):
        peer = lax.rem(my_y + step, n_y)
        push(SPREAD_Y, fr.at[my_y], fr.at[my_y], {"seq": my_z * n_y + peer})

    @pl.when(me > 0)
    def _():
        gone(MG_HALO, mgext.at[0:tokens, :])
        gone(SG_HALO, sgext.at[0:16, :])

    @pl.when(me < n_seq - 1)
    def _():
        gone(SI_HALO, siext.at[tokens : tokens + 16, :])
        gone(MED_HALO, medext.at[0:tokens, :])

    for kind, ref in ((X_OUT, xs), (DG_OUT, ds), (DELTA_BACK, us), (DX_BACK, es)):
        gone(kind, ref.at[0 : (n_seq - 1) * chunk, :])
    gone(CODES, codes_all.at[0 : n_ch - 1])
    gone(CODES_GRAD, cgrad_all.at[0 : n_ch - 1])
    gone(SUM_Y, fg.at[0 : n_y - 1])
    gone(SUM_Z, zr.at[0 : n_z - 1])

    landed(SPREAD_Y, fr.at[0 : n_y - 1])
    gone(SPREAD_Y, fr.at[0 : n_y - 1])
    filter_scale = 1.0 / math.sqrt(tokens * n_seq * size)
    for b in range(blocks):
        rows = slice(b * per_block, (b + 1) * per_block)
        midrange[rows, :] = fr[b, 0:8, :] * (envelope[rows] * filter_scale)
    lines = jnp.concatenate([fr[b, 8:16, :] for b in range(blocks)], axis=1)
    brief[...] = mm_t(of_group, lines, lax.Precision.HIGHEST)[:, 0:short_len] * filter_scale


def on_device(n_y, *arguments):
    x, down, storage = arguments[0], arguments[7], arguments[10]
    short_filter, medium_filter = arguments[11], arguments[12]
    tokens, width = x.shape
    n_seq, n_ch = lax.axis_size("seq"), lax.axis_size("ch")
    cap = max(2, 2 * tokens // n_seq)
    slots, blocks = n_seq * cap, width // LANES
    groups, breadth = short_filter.shape[0], down.shape[1]
    packed = pltpu.VMEM((slots * blocks, LANES), BF16)
    spread = pltpu.VMEM((slots, width), BF16)
    vmem = pl.BlockSpec(memory_space=pltpu.VMEM)
    arguments = list(arguments)
    arguments[10] = storage.reshape(1, n_seq)
    arguments[13] = arguments[13].reshape(1, groups)
    outs = (
        jax.ShapeDtypeStruct((tokens, width), BF16),
        jax.ShapeDtypeStruct((tokens, width), BF16),
        jax.ShapeDtypeStruct((1, breadth, width), F32),
        jax.ShapeDtypeStruct((1, breadth, width), F32),
        jax.ShapeDtypeStruct(short_filter.shape, F32),
        jax.ShapeDtypeStruct(medium_filter.shape, F32),
    )
    return pl.pallas_call(
        functools.partial(kernel, n_seq, n_ch, n_y, cap),
        out_shape=outs,
        in_specs=[vmem] * len(arguments),
        out_specs=[vmem] * len(outs),
        scratch_shapes=[
            pltpu.VMEM((slots * blocks, width), BF16),
            pltpu.VMEM((width, slots * blocks), BF16),
            pltpu.VMEM((2 * LANES, 2 * LANES), BF16),
            pltpu.VMEM((groups, tokens, 2 * tokens), BF16),
            pltpu.VMEM((groups, tokens, 2 * tokens), BF16),
            pltpu.VMEM((2 * tokens, width), BF16),
            pltpu.VMEM((tokens + 16, width), BF16),
            pltpu.VMEM((tokens + 16, width), BF16),
            pltpu.VMEM((2 * tokens, width), BF16),
            packed, packed, packed, packed, packed, packed, packed, packed,
            spread, spread,
            pltpu.VMEM((n_ch, breadth, slots), F32),
            pltpu.VMEM((n_ch, breadth, slots), F32),
            pltpu.VMEM((blocks, 16, LANES), F32),
            pltpu.VMEM((n_y, 16, LANES), F32),
            pltpu.VMEM((n_seq // n_y, 16, LANES), F32),
            pltpu.VMEM((n_y, 16, LANES), F32),
            pltpu.VMEM((groups, LANES), F32),
            pltpu.VMEM((groups, LANES), F32),
            pltpu.SemaphoreType.DMA((13,)),
            pltpu.SemaphoreType.DMA((13,)),
        ],
        compiler_params=pltpu.CompilerParams(
            collective_id=0, has_side_effects=True, vmem_limit_bytes=56 * 1024 * 1024
        ),
    )(*arguments)


def solution(mesh):
    tile, factor = P("seq", "ch"), P("seq", None, "ch")
    return jax.shard_map(
        functools.partial(on_device, 4),
        mesh=mesh,
        in_specs=(tile,) * 7
        + (factor, factor, P("seq", None), P(), P("ch", None), P("ch", None), P("ch")),
        out_specs=(tile, tile, factor, factor, P("ch", None), P("ch", None)),
        check_vma=False,
    )
```

```python
import functools
import math

import jax
import jax.numpy as jnp
from jax import lax
from jax.experimental import pallas as pl
from jax.experimental.pallas import tpu as pltpu
from jax.sharding import PartitionSpec as P

F32, BF16 = jnp.float32, jnp.bfloat16
MESH = pl.DeviceIdType.MESH
LANES = 128
(MG_HALO, SG_HALO, SI_HALO, MED_HALO, X_OUT, DG_OUT, DELTA_BACK, DX_BACK, CODES, CODES_GRAD, SUM_Y, SUM_Z, SPREAD_Y) = range(13)


def mm(left, right):
    return jnp.dot(left, right, preferred_element_type=F32)


def mm_t(left, right, precision=None):
    return lax.dot_general(
        left, right, (((1,), (1,)), ((), ())), precision=precision, preferred_element_type=F32
    )


def t_mm(left, right, precision=None):
    return lax.dot_general(
        left, right, (((0,), (0,)), ((), ())), precision=precision, preferred_element_type=F32
    )


def iota(shape, axis):
    return lax.broadcasted_iota(jnp.int32, shape, axis)


def lane_block(index):
    return pl.ds(pl.multiple_of(index * LANES, LANES), LANES)


def stacked(value):
    return jnp.concatenate(
        [value[:, b * LANES : (b + 1) * LANES] for b in range(value.shape[1] // LANES)], axis=0
    )


def kernel(
    n_seq, n_ch, n_y, cap,
    x, soq, sik, sfv, moq, mik, cot, down, up, clade, storage, short_filter, medium_filter, rate,
    response, dx_out, projector, expander, sums,
    place, place_t, swap, toep_b, toep_f, mgext, sgext, siext, medext,
    xs, xr, ds, dr, us, ur, es, er, yx, yd, codes_all, cgrad_all, fg, yr, zr, fr, taps, mirror,
    send, recv,
):
    tokens, width = x.shape
    blocks = width // LANES
    slots = n_seq * cap
    chunk = blocks * cap
    short_len, groups = short_filter.shape
    per_block = groups // blocks
    size = width // groups
    n_z = n_seq // n_y
    me, mine = lax.axis_index("seq"), lax.axis_index("ch")
    my_z, my_y = me // n_y, lax.rem(me, n_y)

    def push(kind, source, target, device):
        pltpu.make_async_remote_copy(
            src_ref=source, dst_ref=target, send_sem=send.at[kind], recv_sem=recv.at[kind],
            device_id=device, device_id_type=MESH,
        ).start()

    def landed(kind, ref):
        pltpu.make_async_copy(ref, ref, recv.at[kind]).wait()

    def gone(kind, ref):
        pltpu.make_async_copy(ref, ref, send.at[kind]).wait()

    def rows_of(ref, device):
        return ref.at[pl.ds(pl.multiple_of(device * chunk, chunk), chunk), :]

    def partner(turn):
        far = n_seq // 2 - (turn + 1) // 2
        return lax.rem(me + n_seq + far * (2 * lax.rem(turn, 2) - 1), n_seq)

    def exchange(kind, source, target):
        @pl.loop(0, n_seq - 1)
        def _(turn):
            peer = partner(turn)
            push(kind, rows_of(source, peer), rows_of(target, me), {"seq": peer})

        pltpu.make_async_copy(rows_of(source, me), rows_of(target, me), recv.at[kind]).start()

    def share(kind, ref):
        @pl.loop(1, n_ch)
        def _(step):
            peer = lax.rem(mine + step, n_ch)
            push(kind, ref.at[mine], ref.at[mine], {"ch": peer})

    barrier = pltpu.get_barrier_semaphore()

    @pl.loop(0, n_seq - 1)
    def _(turn):
        pl.semaphore_signal(
            barrier, inc=1, device_id={"seq": partner(turn)}, device_id_type=MESH
        )

    @pl.loop(1, n_ch)
    def _(step):
        pl.semaphore_signal(
            barrier, inc=1, device_id={"ch": lax.rem(mine + step, n_ch)}, device_id_type=MESH
        )

    square = (tokens, tokens)
    eye = iota(square, 0) == iota(square, 1)
    clade_row = clade[...].astype(F32)
    clade_col = jnp.sum(jnp.where(eye, clade_row, 0.0), axis=1, keepdims=True)
    earlier = (clade_col == clade_row) & (iota(square, 1) < iota(square, 0))
    rank = jnp.sum(jnp.where(earlier, 1.0, 0.0), axis=1, keepdims=True)
    names = iota((tokens, n_seq), 1).astype(F32)
    owner = jnp.sum(
        jnp.where(clade_col == names, storage[...].astype(F32), 0.0), axis=1, keepdims=True
    )
    key_col = owner * chunk + rank
    key_row = jnp.sum(jnp.where(eye, key_col, 0.0), axis=0, keepdims=True).astype(jnp.int32)
    key_col = key_col.astype(jnp.int32)
    for b in range(blocks):
        lanes = slice(b * LANES, (b + 1) * LANES)
        place[:, lanes] = jnp.where(
            iota((slots * blocks, tokens), 0) == key_row + b * cap, 1.0, 0.0
        ).astype(BF16)
    xs[...] = mm(place[...], stacked(x[...])).astype(BF16)
    mgext[0:tokens, :] = (cot[...].astype(F32) * moq[...].astype(F32)).astype(BF16)

    eye_g = iota((groups, groups), 0) == iota((groups, groups), 1)
    rate_col = jnp.sum(jnp.where(eye_g, rate[...], 0.0), axis=1, keepdims=True)
    envelope = jnp.exp(-rate_col * iota((groups, LANES), 1).astype(F32))
    damped = medium_filter[...] * envelope
    turned = jnp.where(
        iota(square, 0) == lax.rem(tokens - iota(square, 1), tokens), 1.0, 0.0
    ).astype(BF16)
    taps[...] = damped
    mirror[...] = mm(damped.astype(BF16), turned)
    row, col = iota(square, 0), iota(square, 1)

    @pl.loop(0, groups)
    def _(g):
        for source, target, own in ((taps, toep_b, col >= row), (mirror, toep_f, col <= row)):
            wide = jnp.broadcast_to(source[pl.ds(g, 1), :], square)
            band = pltpu.roll(wide, 0, 1, stride=1, stride_axis=0)
            target[g, :, 0:tokens] = jnp.where(own, band, 0.0).astype(BF16)
            target[g, :, tokens : 2 * tokens] = jnp.where(own, 0.0, band).astype(BF16)

    of_group = jnp.where(
        iota((groups, width), 1) // size == iota((groups, width), 0), 1.0, 0.0
    )
    short_wide = jnp.dot(
        short_filter[...], of_group, precision=lax.Precision.HIGHEST, preferred_element_type=F32
    )
    lane_group = iota(square, 1) // size

    for b in range(blocks):
        place_t[b * tokens : (b + 1) * tokens, :] = jnp.where(
            iota((tokens, slots * blocks), 1) == key_col + b * cap, 1.0, 0.0
        ).astype(BF16)

    part = 2 * LANES
    per_part = part // blocks
    at = iota((part, part), 0)
    inside = lax.rem(at, per_part)
    wanted = (inside // cap) * chunk + (at // per_part) * cap + lax.rem(inside, cap)
    swap[...] = jnp.where(iota((part, part), 1) == wanted, 1.0, 0.0).astype(BF16)

    pl.semaphore_wait(barrier, n_seq - 1 + n_ch - 1)

    @pl.when(me > 0)
    def _():
        push(MG_HALO, mgext.at[0:tokens, :], mgext.at[tokens : 2 * tokens, :], {"seq": me - 1})

    exchange(X_OUT, xs, xr)

    def banded(ref, bands, b):
        data = ref[:, lane_block(b)]
        total = jnp.zeros(square, F32)
        for q in range(per_block):
            total = jnp.where(lane_group == q, mm(bands[b * per_block + q], data), total)
        return total

    @pl.when(me < n_seq - 1)
    def _():
        landed(MG_HALO, mgext.at[tokens : 2 * tokens, :])

    @pl.when(me == n_seq - 1)
    def _():
        mgext[tokens : 2 * tokens, :] = jnp.zeros((tokens, width), BF16)

    @pl.loop(0, blocks)
    def _(b):
        lanes = lane_block(b)
        gates = mik[:, lanes].astype(F32) * soq[:, lanes].astype(F32)
        sgext[0:tokens, lanes] = (banded(mgext, toep_b, b) * gates).astype(BF16)

    @pl.when(me > 0)
    def _():
        push(SG_HALO, sgext.at[0:16, :], sgext.at[tokens : tokens + 16, :], {"seq": me - 1})

    def opened(packed, target):
        for p in range(slots // per_part):
            turned_rows = mm(swap[...], packed[p * part : (p + 1) * part, :]).astype(BF16)
            for b in range(blocks):
                target[p * per_part : (p + 1) * per_part, b * LANES : (b + 1) * LANES] = (
                    turned_rows[b * per_part : (b + 1) * per_part]
                )

    def closed(value, packed):
        for p in range(slots // per_part):
            piece = stacked(value[p * per_part : (p + 1) * per_part])
            packed[p * part : (p + 1) * part, :] = t_mm(swap[...], piece).astype(BF16)

    landed(X_OUT, xr)
    opened(xr, yx)
    codes_all[mine] = mm_t(down[0], yx[...])
    share(CODES, codes_all)

    @pl.when(me < n_seq - 1)
    def _():
        landed(SG_HALO, sgext.at[tokens : tokens + 16, :])

    @pl.when(me == n_seq - 1)
    def _():
        sgext[tokens : tokens + 16, :] = jnp.zeros((16, width), BF16)

    ahead = sgext[...].astype(F32)
    total = jnp.zeros((tokens, width), F32)
    for j in range(short_len):
        total = total + short_wide[j : j + 1, :] * ahead[j : j + tokens]
    delta_grad = (0.5 * total * sik[...].astype(F32)).astype(BF16)
    ds[...] = mm(place[...], stacked(delta_grad)).astype(BF16)
    exchange(DG_OUT, ds, dr)

    def summed(ref):
        total = ref[0]
        for c in range(1, ref.shape[0]):
            total = total + ref[c]
        return total

    landed(CODES, codes_all.at[0 : n_ch - 1])
    codes = summed(codes_all).astype(BF16)
    closed((0.5 * t_mm(codes, up[0])).astype(BF16), us)
    exchange(DELTA_BACK, us, ur)

    weight_scale = 1.0 / math.sqrt(tokens)
    landed(DG_OUT, dr)
    opened(dr, yd)
    cgrad_all[mine] = mm_t(up[0], yd[...])
    share(CODES_GRAD, cgrad_all)
    expander[0] = mm(codes, yd[...]) * weight_scale

    landed(DELTA_BACK, ur)
    delta = mm(place_t[...], ur[...]).astype(BF16).astype(F32)
    for b in range(blocks):
        lanes = slice(b * LANES, (b + 1) * LANES)
        siext[16 : 16 + tokens, lanes] = (
            sik[:, lanes].astype(F32)
            * (sfv[:, lanes].astype(F32) + delta[b * tokens : (b + 1) * tokens])
        ).astype(BF16)

    @pl.when(me < n_seq - 1)
    def _():
        push(SI_HALO, siext.at[tokens : tokens + 16, :], siext.at[0:16, :], {"seq": me + 1})

    landed(CODES_GRAD, cgrad_all.at[0 : n_ch - 1])
    codes_grad = summed(cgrad_all).astype(BF16)
    closed(t_mm(codes_grad, down[0]).astype(BF16), es)
    exchange(DX_BACK, es, er)

    @pl.when(me > 0)
    def _():
        landed(SI_HALO, siext.at[0:16, :])

    @pl.when(me == 0)
    def _():
        siext[0:16, :] = jnp.zeros((16, width), BF16)

    behind = siext[...].astype(F32)
    total = jnp.zeros((tokens, width), F32)
    for j in range(short_len):
        total = total + short_wide[j : j + 1, :] * behind[16 - j : 16 - j + tokens]
    medext[0:tokens, :] = (mik[...].astype(F32) * soq[...].astype(F32) * total).astype(BF16)

    @pl.when(me < n_seq - 1)
    def _():
        push(MED_HALO, medext.at[0:tokens, :], medext.at[tokens : 2 * tokens, :], {"seq": me + 1})

    projector[0] = mm(codes_grad, yx[...]) * weight_scale
    short_grad = sgext[0:tokens, :].astype(F32)
    fg[:, 8:16, :] = jnp.zeros((blocks, 8, LANES), F32)
    for j in range(short_len):
        line = jnp.sum(short_grad * behind[16 - j : 16 - j + tokens], axis=0, keepdims=True)
        for b in range(blocks):
            fg[b, 8 + j : 9 + j, :] = line[:, b * LANES : (b + 1) * LANES]

    @pl.when(me > 0)
    def _():
        landed(MED_HALO, medext.at[tokens : 2 * tokens, :])

    @pl.when(me == 0)
    def _():
        medext[tokens : 2 * tokens, :] = jnp.zeros((tokens, width), BF16)

    flip = jnp.where(row + col == tokens - 1, 1.0, 0.0).astype(BF16)

    @pl.loop(0, blocks)
    def _(b):
        lanes = lane_block(b)
        grads = mgext[0:tokens, lanes].astype(F32)
        data = jnp.concatenate(
            [
                mm(flip, medext[0:tokens, lanes]).astype(BF16),
                mm(flip, medext[tokens : 2 * tokens, lanes]).astype(BF16),
            ],
            axis=0,
        )
        for q in range(per_block):
            masked = jnp.where(lane_group == q, grads, 0.0).astype(BF16)
            product = mm_t(masked, data)
            merged = jnp.where(
                col + row >= tokens - 1, product[:, 0:tokens], product[:, tokens : 2 * tokens]
            )
            lined = pltpu.roll(merged, 1, 1, stride=1, stride_axis=0)
            fg[b, q : q + 1, :] = jnp.sum(lined, axis=0, keepdims=True)

    yr[my_y] = fg[my_y]

    @pl.loop(1, n_y)
    def _(step):
        peer = lax.rem(my_y + step, n_y)
        push(SUM_Y, fg.at[peer], yr.at[my_y], {"seq": my_z * n_y + peer})

    def respond(b):
        lanes = lane_block(b)
        response[:, lanes] = (
            banded(medext, toep_f, b) * moq[:, lanes].astype(F32)
        ).astype(BF16)

    @pl.loop(0, blocks // 2)
    def _(b):
        respond(b)

    landed(SUM_Y, yr.at[0 : n_y - 1])
    zr[my_z] = summed(yr)

    @pl.loop(1, n_z)
    def _(step):
        peer = lax.rem(my_z + step, n_z)
        push(SUM_Z, zr.at[my_z], zr.at[my_z], {"seq": peer * n_y + my_y})

    @pl.loop(blocks // 2, blocks)
    def _(b):
        respond(b)

    landed(DX_BACK, er)
    back = mm(place_t[...], er[...]).astype(BF16)
    for b in range(blocks):
        dx_out[:, b * LANES : (b + 1) * LANES] = back[b * tokens : (b + 1) * tokens]

    landed(SUM_Z, zr.at[0 : n_z - 1])
    fr[my_y] = summed(zr)

    @pl.loop(1, n_y)
    def _(step):
        peer = lax.rem(my_y + step, n_y)
        push(SPREAD_Y, fr.at[my_y], fr.at[my_y], {"seq": my_z * n_y + peer})

    @pl.when(me > 0)
    def _():
        gone(MG_HALO, mgext.at[0:tokens, :])
        gone(SG_HALO, sgext.at[0:16, :])

    @pl.when(me < n_seq - 1)
    def _():
        gone(SI_HALO, siext.at[tokens : tokens + 16, :])
        gone(MED_HALO, medext.at[0:tokens, :])

    for kind, ref in ((X_OUT, xs), (DG_OUT, ds), (DELTA_BACK, us), (DX_BACK, es)):
        gone(kind, ref.at[0 : (n_seq - 1) * chunk, :])
    gone(CODES, codes_all.at[0 : n_ch - 1])
    gone(CODES_GRAD, cgrad_all.at[0 : n_ch - 1])
    gone(SUM_Y, fg.at[0 : n_y - 1])
    gone(SUM_Z, zr.at[0 : n_z - 1])

    landed(SPREAD_Y, fr.at[0 : n_y - 1])
    gone(SPREAD_Y, fr.at[0 : n_y - 1])
    sums[...] = fr[...]


def finish(
    n_seq, response, dx, projector, expander, sums, rate,
    response_out, dx_out, projector_out, expander_out, brief, midrange,
):
    tokens, width = response.shape
    short_len, groups = brief.shape
    blocks, per_block, size = sums.shape[0], groups // sums.shape[0], width // groups
    response_out[...] = response[...]
    dx_out[...] = dx[...]
    projector_out[...] = projector[...]
    expander_out[...] = expander[...]
    eye = iota((groups, groups), 0) == iota((groups, groups), 1)
    rate_col = jnp.sum(jnp.where(eye, rate[...], 0.0), axis=1, keepdims=True)
    envelope = jnp.exp(-rate_col * iota((groups, LANES), 1).astype(F32))
    scale = 1.0 / math.sqrt(tokens * n_seq * size)
    for b in range(blocks):
        rows = slice(b * per_block, (b + 1) * per_block)
        midrange[rows, :] = sums[b, 0:8, :] * (envelope[rows] * scale)
    of_group = jnp.where(
        iota((groups, width), 1) // size == iota((groups, width), 0), 1.0, 0.0
    )
    lines = jnp.concatenate([sums[b, 8:16, :] for b in range(blocks)], axis=1)
    brief[...] = mm_t(lines, of_group, lax.Precision.HIGHEST)[0:short_len] * scale


def on_device(n_y, *arguments):
    x, down, storage = arguments[0], arguments[7], arguments[10]
    short_filter, medium_filter = arguments[11], arguments[12]
    tokens, width = x.shape
    n_seq, n_ch = lax.axis_size("seq"), lax.axis_size("ch")
    cap = max(2, 2 * tokens // n_seq)
    slots, blocks = n_seq * cap, width // LANES
    groups, breadth = short_filter.shape[0], down.shape[1]
    packed = pltpu.VMEM((slots * blocks, LANES), BF16)
    spread = pltpu.VMEM((slots, width), BF16)
    vmem = pl.BlockSpec(memory_space=pltpu.VMEM)
    arguments = list(arguments)
    arguments[9] = arguments[9].T
    arguments[10] = storage.reshape(1, n_seq)
    arguments[11] = short_filter.T
    arguments[13] = arguments[13].reshape(1, groups)
    outs = (
        jax.ShapeDtypeStruct((tokens, width), BF16),
        jax.ShapeDtypeStruct((tokens, width), BF16),
        jax.ShapeDtypeStruct((1, breadth, width), F32),
        jax.ShapeDtypeStruct((1, breadth, width), F32),
    )
    filters = (
        jax.ShapeDtypeStruct(short_filter.shape[::-1], F32),
        jax.ShapeDtypeStruct(medium_filter.shape, F32),
    )
    results = pl.pallas_call(
        functools.partial(kernel, n_seq, n_ch, n_y, cap),
        out_shape=outs + (jax.ShapeDtypeStruct((blocks, 16, LANES), F32),),
        in_specs=[vmem] * len(arguments),
        out_specs=[vmem] * (len(outs) + 1),
        scratch_shapes=[
            pltpu.VMEM((slots * blocks, width), BF16),
            pltpu.VMEM((width, slots * blocks), BF16),
            pltpu.VMEM((2 * LANES, 2 * LANES), BF16),
            pltpu.VMEM((groups, tokens, 2 * tokens), BF16),
            pltpu.VMEM((groups, tokens, 2 * tokens), BF16),
            pltpu.VMEM((2 * tokens, width), BF16),
            pltpu.VMEM((tokens + 16, width), BF16),
            pltpu.VMEM((tokens + 16, width), BF16),
            pltpu.VMEM((2 * tokens, width), BF16),
            packed, packed, packed, packed, packed, packed, packed, packed,
            spread, spread,
            pltpu.VMEM((n_ch, breadth, slots), F32),
            pltpu.VMEM((n_ch, breadth, slots), F32),
            pltpu.VMEM((blocks, 16, LANES), F32),
            pltpu.VMEM((n_y, 16, LANES), F32),
            pltpu.VMEM((n_seq // n_y, 16, LANES), F32),
            pltpu.VMEM((n_y, 16, LANES), F32),
            pltpu.VMEM((groups, LANES), F32),
            pltpu.VMEM((groups, LANES), F32),
            pltpu.SemaphoreType.DMA((13,)),
            pltpu.SemaphoreType.DMA((13,)),
        ],
        compiler_params=pltpu.CompilerParams(
            collective_id=0, has_side_effects=True, vmem_limit_bytes=56 * 1024 * 1024
        ),
    )(*arguments)
    *results, brief, midrange = pl.pallas_call(
        functools.partial(finish, n_seq),
        out_shape=outs + filters,
        in_specs=[vmem] * 6,
        out_specs=[vmem] * 6,
    )(*results, arguments[13])
    return (*results, brief.T, midrange)


def solution(mesh):
    tile, factor = P("seq", "ch"), P("seq", None, "ch")
    return jax.shard_map(
        functools.partial(on_device, 4),
        mesh=mesh,
        in_specs=(tile,) * 7
        + (factor, factor, P("seq", None), P(), P("ch", None), P("ch", None), P("ch")),
        out_specs=(tile, tile, factor, factor, P("ch", None), P("ch", None)),
        check_vma=False,
    )
```

```python
import functools
import math

import jax
import jax.numpy as jnp
from jax import lax
from jax.experimental import pallas as pl
from jax.experimental.pallas import tpu as pltpu
from jax.sharding import PartitionSpec as P

F32, BF16 = jnp.float32, jnp.bfloat16
MESH = pl.DeviceIdType.MESH
LANES = 128
(MG_HALO, SG_HALO, SI_HALO, MED_HALO, X_OUT, DG_OUT, DELTA_BACK, DX_BACK, CODES, CODES_GRAD, SUM_Y, SUM_Z, SPREAD_Y) = range(13)


def mm(left, right):
    return jnp.dot(left, right, preferred_element_type=F32)


def mm_t(left, right, precision=None):
    return lax.dot_general(
        left, right, (((1,), (1,)), ((), ())), precision=precision, preferred_element_type=F32
    )


def t_mm(left, right, precision=None):
    return lax.dot_general(
        left, right, (((0,), (0,)), ((), ())), precision=precision, preferred_element_type=F32
    )


def iota(shape, axis):
    return lax.broadcasted_iota(jnp.int32, shape, axis)


def lane_block(index):
    return pl.ds(pl.multiple_of(index * LANES, LANES), LANES)


def stacked(value):
    return jnp.concatenate(
        [value[:, b * LANES : (b + 1) * LANES] for b in range(value.shape[1] // LANES)], axis=0
    )


def kernel(
    n_seq, n_ch, n_y, cap,
    x, soq, sik, sfv, moq, mik, cot, down, up, clade, storage, short_filter, medium_filter, rate,
    response, dx_out, projector, expander, sums,
    place, place_t, swap, toep_b, toep_f, mgext, sgext, siext, medext,
    xs, xr, ds, dr, us, ur, es, er, yx, yd, codes_all, cgrad_all, fg, yr, zr, fr, taps, mirror,
    send, recv,
):
    tokens, width = x.shape
    blocks = width // LANES
    slots = n_seq * cap
    chunk = blocks * cap
    short_len, groups = short_filter.shape
    per_block = groups // blocks
    size = width // groups
    n_z = n_seq // n_y
    me, mine = lax.axis_index("seq"), lax.axis_index("ch")
    my_z, my_y = me // n_y, lax.rem(me, n_y)

    def push(kind, source, target, device):
        pltpu.make_async_remote_copy(
            src_ref=source, dst_ref=target, send_sem=send.at[kind], recv_sem=recv.at[kind],
            device_id=device, device_id_type=MESH,
        ).start()

    def landed(kind, ref):
        pltpu.make_async_copy(ref, ref, recv.at[kind]).wait()

    def gone(kind, ref):
        pltpu.make_async_copy(ref, ref, send.at[kind]).wait()

    def rows_of(ref, device):
        return ref.at[pl.ds(pl.multiple_of(device * chunk, chunk), chunk), :]

    def partner(turn):
        far = n_seq // 2 - (turn + 1) // 2
        return lax.rem(me + n_seq + far * (2 * lax.rem(turn, 2) - 1), n_seq)

    def exchange(kind, source, target, first=0, last=n_seq - 1):
        @pl.loop(first, last)
        def _(turn):
            peer = partner(turn)
            push(kind, rows_of(source, peer), rows_of(target, me), {"seq": peer})

        if last == n_seq - 1:
            pltpu.make_async_copy(rows_of(source, me), rows_of(target, me), recv.at[kind]).start()

    def share(kind, ref):
        @pl.loop(1, n_ch)
        def _(step):
            peer = lax.rem(mine + step, n_ch)
            push(kind, ref.at[mine], ref.at[mine], {"ch": peer})

    barrier = pltpu.get_barrier_semaphore()

    @pl.loop(0, n_seq - 1)
    def _(turn):
        pl.semaphore_signal(
            barrier, inc=1, device_id={"seq": partner(turn)}, device_id_type=MESH
        )

    @pl.loop(1, n_ch)
    def _(step):
        pl.semaphore_signal(
            barrier, inc=1, device_id={"ch": lax.rem(mine + step, n_ch)}, device_id_type=MESH
        )

    square = (tokens, tokens)
    eye = iota(square, 0) == iota(square, 1)
    clade_row = clade[...].astype(F32)
    clade_col = jnp.sum(jnp.where(eye, clade_row, 0.0), axis=1, keepdims=True)
    earlier = (clade_col == clade_row) & (iota(square, 1) < iota(square, 0))
    rank = jnp.sum(jnp.where(earlier, 1.0, 0.0), axis=1, keepdims=True)
    names = iota((tokens, n_seq), 1).astype(F32)
    owner = jnp.sum(
        jnp.where(clade_col == names, storage[...].astype(F32), 0.0), axis=1, keepdims=True
    )
    key_col = owner * chunk + rank
    key_row = jnp.sum(jnp.where(eye, key_col, 0.0), axis=0, keepdims=True).astype(jnp.int32)
    key_col = key_col.astype(jnp.int32)
    for b in range(blocks):
        lanes = slice(b * LANES, (b + 1) * LANES)
        place[:, lanes] = jnp.where(
            iota((slots * blocks, tokens), 0) == key_row + b * cap, 1.0, 0.0
        ).astype(BF16)
    xs[...] = mm(place[...], stacked(x[...])).astype(BF16)
    mgext[0:tokens, :] = (cot[...].astype(F32) * moq[...].astype(F32)).astype(BF16)

    eye_g = iota((groups, groups), 0) == iota((groups, groups), 1)
    rate_col = jnp.sum(jnp.where(eye_g, rate[...], 0.0), axis=1, keepdims=True)
    envelope = jnp.exp(-rate_col * iota((groups, LANES), 1).astype(F32))
    damped = medium_filter[...] * envelope
    turned = jnp.where(
        iota(square, 0) == lax.rem(tokens - iota(square, 1), tokens), 1.0, 0.0
    ).astype(BF16)
    taps[...] = damped
    mirror[...] = mm(damped.astype(BF16), turned)
    row, col = iota(square, 0), iota(square, 1)

    @pl.loop(0, groups)
    def _(g):
        for source, target, own in ((taps, toep_b, col >= row), (mirror, toep_f, col <= row)):
            wide = jnp.broadcast_to(source[pl.ds(g, 1), :], square)
            band = pltpu.roll(wide, 0, 1, stride=1, stride_axis=0)
            target[g, :, 0:tokens] = jnp.where(own, band, 0.0).astype(BF16)
            target[g, :, tokens : 2 * tokens] = jnp.where(own, 0.0, band).astype(BF16)

    of_group = jnp.where(
        iota((groups, width), 1) // size == iota((groups, width), 0), 1.0, 0.0
    )
    short_wide = jnp.dot(
        short_filter[...], of_group, precision=lax.Precision.HIGHEST, preferred_element_type=F32
    )
    lane_group = iota(square, 1) // size

    for b in range(blocks):
        place_t[b * tokens : (b + 1) * tokens, :] = jnp.where(
            iota((tokens, slots * blocks), 1) == key_col + b * cap, 1.0, 0.0
        ).astype(BF16)

    part = 2 * LANES
    per_part = part // blocks
    at = iota((part, part), 0)
    inside = lax.rem(at, per_part)
    wanted = (inside // cap) * chunk + (at // per_part) * cap + lax.rem(inside, cap)
    swap[...] = jnp.where(iota((part, part), 1) == wanted, 1.0, 0.0).astype(BF16)

    pl.semaphore_wait(barrier, n_seq - 1 + n_ch - 1)

    @pl.when(me > 0)
    def _():
        push(MG_HALO, mgext.at[0:tokens, :], mgext.at[tokens : 2 * tokens, :], {"seq": me - 1})

    exchange(X_OUT, xs, xr)

    def banded(ref, bands, b):
        data = ref[:, lane_block(b)]
        total = jnp.zeros(square, F32)
        for q in range(per_block):
            total = jnp.where(lane_group == q, mm(bands[b * per_block + q], data), total)
        return total

    @pl.when(me < n_seq - 1)
    def _():
        landed(MG_HALO, mgext.at[tokens : 2 * tokens, :])

    @pl.when(me == n_seq - 1)
    def _():
        mgext[tokens : 2 * tokens, :] = jnp.zeros((tokens, width), BF16)

    @pl.loop(0, blocks)
    def _(b):
        lanes = lane_block(b)
        gates = mik[:, lanes].astype(F32) * soq[:, lanes].astype(F32)
        sgext[0:tokens, lanes] = (banded(mgext, toep_b, b) * gates).astype(BF16)

    @pl.when(me > 0)
    def _():
        push(SG_HALO, sgext.at[0:16, :], sgext.at[tokens : tokens + 16, :], {"seq": me - 1})

    def opened(packed, target):
        for p in range(slots // per_part):
            turned_rows = mm(swap[...], packed[p * part : (p + 1) * part, :]).astype(BF16)
            for b in range(blocks):
                target[p * per_part : (p + 1) * per_part, b * LANES : (b + 1) * LANES] = (
                    turned_rows[b * per_part : (b + 1) * per_part]
                )

    def closed(value, packed):
        for p in range(slots // per_part):
            piece = stacked(value[p * per_part : (p + 1) * per_part])
            packed[p * part : (p + 1) * part, :] = t_mm(swap[...], piece).astype(BF16)

    landed(X_OUT, xr)
    opened(xr, yx)
    codes_all[mine] = mm_t(down[0], yx[...])
    share(CODES, codes_all)

    @pl.when(me < n_seq - 1)
    def _():
        landed(SG_HALO, sgext.at[tokens : tokens + 16, :])

    @pl.when(me == n_seq - 1)
    def _():
        sgext[tokens : tokens + 16, :] = jnp.zeros((16, width), BF16)

    ahead = sgext[...].astype(F32)
    total = jnp.zeros((tokens, width), F32)
    for j in range(short_len):
        total = total + short_wide[j : j + 1, :] * ahead[j : j + tokens]
    delta_grad = (0.5 * total * sik[...].astype(F32)).astype(BF16)
    ds[...] = mm(place[...], stacked(delta_grad)).astype(BF16)
    split = 3 * n_seq // 8
    exchange(DG_OUT, ds, dr, first=split)

    def summed(ref):
        total = ref[0]
        for c in range(1, ref.shape[0]):
            total = total + ref[c]
        return total

    landed(CODES, codes_all.at[0 : n_ch - 1])
    codes = summed(codes_all).astype(BF16)
    closed((0.5 * t_mm(codes, up[0])).astype(BF16), us)
    exchange(DELTA_BACK, us, ur)
    exchange(DG_OUT, ds, dr, last=split)

    landed(DELTA_BACK, ur)
    delta = mm(place_t[...], ur[...]).astype(BF16).astype(F32)
    for b in range(blocks):
        lanes = slice(b * LANES, (b + 1) * LANES)
        siext[16 : 16 + tokens, lanes] = (
            sik[:, lanes].astype(F32)
            * (sfv[:, lanes].astype(F32) + delta[b * tokens : (b + 1) * tokens])
        ).astype(BF16)

    @pl.when(me < n_seq - 1)
    def _():
        push(SI_HALO, siext.at[tokens : tokens + 16, :], siext.at[0:16, :], {"seq": me + 1})

    @pl.when(me > 0)
    def _():
        landed(SI_HALO, siext.at[0:16, :])

    @pl.when(me == 0)
    def _():
        siext[0:16, :] = jnp.zeros((16, width), BF16)

    behind = siext[...].astype(F32)
    total = jnp.zeros((tokens, width), F32)
    for j in range(short_len):
        total = total + short_wide[j : j + 1, :] * behind[16 - j : 16 - j + tokens]
    medext[0:tokens, :] = (mik[...].astype(F32) * soq[...].astype(F32) * total).astype(BF16)

    @pl.when(me < n_seq - 1)
    def _():
        push(MED_HALO, medext.at[0:tokens, :], medext.at[tokens : 2 * tokens, :], {"seq": me + 1})

    short_grad = sgext[0:tokens, :].astype(F32)
    fg[:, 8:16, :] = jnp.zeros((blocks, 8, LANES), F32)
    for j in range(short_len):
        line = jnp.sum(short_grad * behind[16 - j : 16 - j + tokens], axis=0, keepdims=True)
        for b in range(blocks):
            fg[b, 8 + j : 9 + j, :] = line[:, b * LANES : (b + 1) * LANES]

    @pl.when(me > 0)
    def _():
        landed(MED_HALO, medext.at[tokens : 2 * tokens, :])

    @pl.when(me == 0)
    def _():
        medext[tokens : 2 * tokens, :] = jnp.zeros((tokens, width), BF16)

    flip = jnp.where(row + col == tokens - 1, 1.0, 0.0).astype(BF16)

    @pl.loop(0, blocks)
    def _(b):
        lanes = lane_block(b)
        grads = mgext[0:tokens, lanes].astype(F32)
        data = jnp.concatenate(
            [
                mm(flip, medext[0:tokens, lanes]).astype(BF16),
                mm(flip, medext[tokens : 2 * tokens, lanes]).astype(BF16),
            ],
            axis=0,
        )
        for q in range(per_block):
            masked = jnp.where(lane_group == q, grads, 0.0).astype(BF16)
            product = mm_t(masked, data)
            merged = jnp.where(
                col + row >= tokens - 1, product[:, 0:tokens], product[:, tokens : 2 * tokens]
            )
            lined = pltpu.roll(merged, 1, 1, stride=1, stride_axis=0)
            fg[b, q : q + 1, :] = jnp.sum(lined, axis=0, keepdims=True)

    yr[my_y] = fg[my_y]

    @pl.loop(1, n_y)
    def _(step):
        peer = lax.rem(my_y + step, n_y)
        push(SUM_Y, fg.at[peer], yr.at[my_y], {"seq": my_z * n_y + peer})

    def respond(b):
        lanes = lane_block(b)
        response[:, lanes] = (
            banded(medext, toep_f, b) * moq[:, lanes].astype(F32)
        ).astype(BF16)

    landed(DG_OUT, dr)
    opened(dr, yd)
    cgrad_all[mine] = mm_t(up[0], yd[...])
    share(CODES_GRAD, cgrad_all)

    @pl.loop(0, blocks // 2)
    def _(b):
        respond(b)

    landed(SUM_Y, yr.at[0 : n_y - 1])
    zr[my_z] = summed(yr)

    @pl.loop(1, n_z)
    def _(step):
        peer = lax.rem(my_z + step, n_z)
        push(SUM_Z, zr.at[my_z], zr.at[my_z], {"seq": peer * n_y + my_y})

    landed(CODES_GRAD, cgrad_all.at[0 : n_ch - 1])
    codes_grad = summed(cgrad_all).astype(BF16)
    closed(t_mm(codes_grad, down[0]).astype(BF16), es)
    exchange(DX_BACK, es, er)

    @pl.loop(blocks // 2, blocks)
    def _(b):
        respond(b)

    landed(SUM_Z, zr.at[0 : n_z - 1])
    fr[my_y] = summed(zr)

    @pl.loop(1, n_y)
    def _(step):
        peer = lax.rem(my_y + step, n_y)
        push(SPREAD_Y, fr.at[my_y], fr.at[my_y], {"seq": my_z * n_y + peer})

    weight_scale = 1.0 / math.sqrt(tokens)
    expander[0] = mm(codes, yd[...]) * weight_scale
    projector[0] = mm(codes_grad, yx[...]) * weight_scale

    landed(DX_BACK, er)
    back = mm(place_t[...], er[...]).astype(BF16)
    for b in range(blocks):
        dx_out[:, b * LANES : (b + 1) * LANES] = back[b * tokens : (b + 1) * tokens]

    @pl.when(me > 0)
    def _():
        gone(MG_HALO, mgext.at[0:tokens, :])
        gone(SG_HALO, sgext.at[0:16, :])

    @pl.when(me < n_seq - 1)
    def _():
        gone(SI_HALO, siext.at[tokens : tokens + 16, :])
        gone(MED_HALO, medext.at[0:tokens, :])

    for kind, ref in ((X_OUT, xs), (DG_OUT, ds), (DELTA_BACK, us), (DX_BACK, es)):
        gone(kind, ref.at[0 : (n_seq - 1) * chunk, :])
    gone(CODES, codes_all.at[0 : n_ch - 1])
    gone(CODES_GRAD, cgrad_all.at[0 : n_ch - 1])
    gone(SUM_Y, fg.at[0 : n_y - 1])
    gone(SUM_Z, zr.at[0 : n_z - 1])

    landed(SPREAD_Y, fr.at[0 : n_y - 1])
    gone(SPREAD_Y, fr.at[0 : n_y - 1])
    sums[...] = fr[...]


def finish(
    n_seq, response, dx, projector, expander, sums, rate,
    response_out, dx_out, projector_out, expander_out, brief, midrange,
):
    tokens, width = response.shape
    short_len, groups = brief.shape
    blocks, per_block, size = sums.shape[0], groups // sums.shape[0], width // groups
    response_out[...] = response[...]
    dx_out[...] = dx[...]
    projector_out[...] = projector[...]
    expander_out[...] = expander[...]
    eye = iota((groups, groups), 0) == iota((groups, groups), 1)
    rate_col = jnp.sum(jnp.where(eye, rate[...], 0.0), axis=1, keepdims=True)
    envelope = jnp.exp(-rate_col * iota((groups, LANES), 1).astype(F32))
    scale = 1.0 / math.sqrt(tokens * n_seq * size)
    for b in range(blocks):
        rows = slice(b * per_block, (b + 1) * per_block)
        midrange[rows, :] = sums[b, 0:8, :] * (envelope[rows] * scale)
    of_group = jnp.where(
        iota((groups, width), 1) // size == iota((groups, width), 0), 1.0, 0.0
    )
    lines = jnp.concatenate([sums[b, 8:16, :] for b in range(blocks)], axis=1)
    brief[...] = mm_t(lines, of_group, lax.Precision.HIGHEST)[0:short_len] * scale


def on_device(n_y, *arguments):
    x, down, storage = arguments[0], arguments[7], arguments[10]
    short_filter, medium_filter = arguments[11], arguments[12]
    tokens, width = x.shape
    n_seq, n_ch = lax.axis_size("seq"), lax.axis_size("ch")
    cap = max(2, 2 * tokens // n_seq)
    slots, blocks = n_seq * cap, width // LANES
    groups, breadth = short_filter.shape[0], down.shape[1]
    packed = pltpu.VMEM((slots * blocks, LANES), BF16)
    spread = pltpu.VMEM((slots, width), BF16)
    vmem = pl.BlockSpec(memory_space=pltpu.VMEM)
    arguments = list(arguments)
    arguments[9] = arguments[9].T
    arguments[10] = storage.reshape(1, n_seq)
    arguments[11] = short_filter.T
    arguments[13] = arguments[13].reshape(1, groups)
    outs = (
        jax.ShapeDtypeStruct((tokens, width), BF16),
        jax.ShapeDtypeStruct((tokens, width), BF16),
        jax.ShapeDtypeStruct((1, breadth, width), F32),
        jax.ShapeDtypeStruct((1, breadth, width), F32),
    )
    filters = (
        jax.ShapeDtypeStruct(short_filter.shape[::-1], F32),
        jax.ShapeDtypeStruct(medium_filter.shape, F32),
    )
    results = pl.pallas_call(
        functools.partial(kernel, n_seq, n_ch, n_y, cap),
        out_shape=outs + (jax.ShapeDtypeStruct((blocks, 16, LANES), F32),),
        in_specs=[vmem] * len(arguments),
        out_specs=[vmem] * (len(outs) + 1),
        scratch_shapes=[
            pltpu.VMEM((slots * blocks, width), BF16),
            pltpu.VMEM((width, slots * blocks), BF16),
            pltpu.VMEM((2 * LANES, 2 * LANES), BF16),
            pltpu.VMEM((groups, tokens, 2 * tokens), BF16),
            pltpu.VMEM((groups, tokens, 2 * tokens), BF16),
            pltpu.VMEM((2 * tokens, width), BF16),
            pltpu.VMEM((tokens + 16, width), BF16),
            pltpu.VMEM((tokens + 16, width), BF16),
            pltpu.VMEM((2 * tokens, width), BF16),
            packed, packed, packed, packed, packed, packed, packed, packed,
            spread, spread,
            pltpu.VMEM((n_ch, breadth, slots), F32),
            pltpu.VMEM((n_ch, breadth, slots), F32),
            pltpu.VMEM((blocks, 16, LANES), F32),
            pltpu.VMEM((n_y, 16, LANES), F32),
            pltpu.VMEM((n_seq // n_y, 16, LANES), F32),
            pltpu.VMEM((n_y, 16, LANES), F32),
            pltpu.VMEM((groups, LANES), F32),
            pltpu.VMEM((groups, LANES), F32),
            pltpu.SemaphoreType.DMA((13,)),
            pltpu.SemaphoreType.DMA((13,)),
        ],
        compiler_params=pltpu.CompilerParams(
            collective_id=0, has_side_effects=True, vmem_limit_bytes=56 * 1024 * 1024
        ),
    )(*arguments)
    *results, brief, midrange = pl.pallas_call(
        functools.partial(finish, n_seq),
        out_shape=outs + filters,
        in_specs=[vmem] * 6,
        out_specs=[vmem] * 6,
    )(*results, arguments[13])
    return (*results, brief.T, midrange)


def solution(mesh):
    tile, factor = P("seq", "ch"), P("seq", None, "ch")
    return jax.shard_map(
        functools.partial(on_device, 4),
        mesh=mesh,
        in_specs=(tile,) * 7
        + (factor, factor, P("seq", None), P(), P("ch", None), P("ch", None), P("ch")),
        out_specs=(tile, tile, factor, factor, P("ch", None), P("ch", None)),
        check_vma=False,
    )
```

```python
import functools
import math

import jax
import jax.numpy as jnp
from jax import lax
from jax.experimental import pallas as pl
from jax.experimental.pallas import tpu as pltpu
from jax.sharding import PartitionSpec as P

F32, BF16 = jnp.float32, jnp.bfloat16
MESH = pl.DeviceIdType.MESH
LANES = 128
(MG_HALO, SG_HALO, SI_HALO, MED_HALO, X_OUT, DG_OUT, DELTA_BACK, DX_BACK, CODES, CODES_GRAD, SUM_Y, SUM_Z, SPREAD_Y) = range(13)


def mm(left, right):
    return jnp.dot(left, right, preferred_element_type=F32)


def mm_t(left, right, precision=None):
    return lax.dot_general(
        left, right, (((1,), (1,)), ((), ())), precision=precision, preferred_element_type=F32
    )


def t_mm(left, right, precision=None):
    return lax.dot_general(
        left, right, (((0,), (0,)), ((), ())), precision=precision, preferred_element_type=F32
    )


def iota(shape, axis):
    return lax.broadcasted_iota(jnp.int32, shape, axis)


def lane_block(index):
    return pl.ds(pl.multiple_of(index * LANES, LANES), LANES)


def stacked(value):
    return jnp.concatenate(
        [value[:, b * LANES : (b + 1) * LANES] for b in range(value.shape[1] // LANES)], axis=0
    )


def kernel(
    n_seq, n_ch, n_y, cap,
    x, soq, sik, sfv, moq, mik, cot, down, up, clade, storage, short_filter, medium_filter, rate,
    response, dx_out, projector, expander, sums,
    place, place_t, swap, toep_b, toep_f, mgext, sgext, siext, medext,
    xs, xr, ds, dr, us, ur, es, er, yx, yd, codes_all, cgrad_all, fg, yr, zr, fr, taps, mirror,
    send, recv,
):
    tokens, width = x.shape
    blocks = width // LANES
    slots = n_seq * cap
    chunk = blocks * cap
    short_len, groups = short_filter.shape
    per_block = groups // blocks
    size = width // groups
    n_z = n_seq // n_y
    me, mine = lax.axis_index("seq"), lax.axis_index("ch")
    my_z, my_y = me // n_y, lax.rem(me, n_y)

    def push(kind, source, target, device):
        pltpu.make_async_remote_copy(
            src_ref=source, dst_ref=target, send_sem=send.at[kind], recv_sem=recv.at[kind],
            device_id=device, device_id_type=MESH,
        ).start()

    def landed(kind, ref):
        pltpu.make_async_copy(ref, ref, recv.at[kind]).wait()

    def gone(kind, ref):
        pltpu.make_async_copy(ref, ref, send.at[kind]).wait()

    def rows_of(ref, device):
        return ref.at[pl.ds(pl.multiple_of(device * chunk, chunk), chunk), :]

    def partner(turn):
        far = n_seq // 2 - (turn + 1) // 2
        return lax.rem(me + n_seq + far * (2 * lax.rem(turn, 2) - 1), n_seq)

    def exchange(kind, source, target, first=0, last=n_seq - 1):
        @pl.loop(first, last)
        def _(turn):
            peer = partner(turn)
            push(kind, rows_of(source, peer), rows_of(target, me), {"seq": peer})

        if last == n_seq - 1:
            pltpu.make_async_copy(rows_of(source, me), rows_of(target, me), recv.at[kind]).start()

    def share(kind, ref):
        @pl.loop(1, n_ch)
        def _(step):
            peer = lax.rem(mine + step, n_ch)
            push(kind, ref.at[mine], ref.at[mine], {"ch": peer})

    barrier = pltpu.get_barrier_semaphore()

    @pl.loop(0, n_seq - 1)
    def _(turn):
        pl.semaphore_signal(
            barrier, inc=1, device_id={"seq": partner(turn)}, device_id_type=MESH
        )

    @pl.loop(1, n_ch)
    def _(step):
        pl.semaphore_signal(
            barrier, inc=1, device_id={"ch": lax.rem(mine + step, n_ch)}, device_id_type=MESH
        )

    square = (tokens, tokens)
    eye = iota(square, 0) == iota(square, 1)
    clade_row = clade[...].astype(F32)
    clade_col = jnp.sum(jnp.where(eye, clade_row, 0.0), axis=1, keepdims=True)
    earlier = (clade_col == clade_row) & (iota(square, 1) < iota(square, 0))
    rank = jnp.sum(jnp.where(earlier, 1.0, 0.0), axis=1, keepdims=True)
    names = iota((tokens, n_seq), 1).astype(F32)
    owner = jnp.sum(
        jnp.where(clade_col == names, storage[...].astype(F32), 0.0), axis=1, keepdims=True
    )
    key_col = owner * chunk + rank
    key_row = jnp.sum(jnp.where(eye, key_col, 0.0), axis=0, keepdims=True).astype(jnp.int32)
    key_col = key_col.astype(jnp.int32)
    for b in range(blocks):
        lanes = slice(b * LANES, (b + 1) * LANES)
        place[:, lanes] = jnp.where(
            iota((slots * blocks, tokens), 0) == key_row + b * cap, 1.0, 0.0
        ).astype(BF16)
    xs[...] = mm(place[...], stacked(x[...])).astype(BF16)
    mgext[0:tokens, :] = (cot[...].astype(F32) * moq[...].astype(F32)).astype(BF16)

    eye_g = iota((groups, groups), 0) == iota((groups, groups), 1)
    rate_col = jnp.sum(jnp.where(eye_g, rate[...], 0.0), axis=1, keepdims=True)
    envelope = jnp.exp(-rate_col * iota((groups, LANES), 1).astype(F32))
    damped = medium_filter[...] * envelope
    turned = jnp.where(
        iota(square, 0) == lax.rem(tokens - iota(square, 1), tokens), 1.0, 0.0
    ).astype(BF16)
    taps[...] = damped
    mirror[...] = mm(damped.astype(BF16), turned)
    row, col = iota(square, 0), iota(square, 1)

    @pl.loop(0, groups)
    def _(g):
        for source, target, own in ((taps, toep_b, col >= row), (mirror, toep_f, col <= row)):
            wide = jnp.broadcast_to(source[pl.ds(g, 1), :], square)
            band = pltpu.roll(wide, 0, 1, stride=1, stride_axis=0)
            target[g, :, 0:tokens] = jnp.where(own, band, 0.0).astype(BF16)
            target[g, :, tokens : 2 * tokens] = jnp.where(own, 0.0, band).astype(BF16)

    of_group = jnp.where(
        iota((groups, width), 1) // size == iota((groups, width), 0), 1.0, 0.0
    )
    short_wide = jnp.dot(
        short_filter[...], of_group, precision=lax.Precision.HIGHEST, preferred_element_type=F32
    )
    lane_group = iota(square, 1) // size

    for b in range(blocks):
        place_t[b * tokens : (b + 1) * tokens, :] = jnp.where(
            iota((tokens, slots * blocks), 1) == key_col + b * cap, 1.0, 0.0
        ).astype(BF16)

    part = 2 * LANES
    per_part = part // blocks
    at = iota((part, part), 0)
    inside = lax.rem(at, per_part)
    wanted = (inside // cap) * chunk + (at // per_part) * cap + lax.rem(inside, cap)
    swap[...] = jnp.where(iota((part, part), 1) == wanted, 1.0, 0.0).astype(BF16)

    pl.semaphore_wait(barrier, n_seq - 1 + n_ch - 1)

    @pl.when(me > 0)
    def _():
        push(MG_HALO, mgext.at[0:tokens, :], mgext.at[tokens : 2 * tokens, :], {"seq": me - 1})

    exchange(X_OUT, xs, xr)

    def banded(ref, bands, b):
        data = ref[:, lane_block(b)]
        total = jnp.zeros(square, F32)
        for q in range(per_block):
            total = jnp.where(lane_group == q, mm(bands[b * per_block + q], data), total)
        return total

    @pl.when(me < n_seq - 1)
    def _():
        landed(MG_HALO, mgext.at[tokens : 2 * tokens, :])

    @pl.when(me == n_seq - 1)
    def _():
        mgext[tokens : 2 * tokens, :] = jnp.zeros((tokens, width), BF16)

    @pl.loop(0, blocks)
    def _(b):
        lanes = lane_block(b)
        gates = mik[:, lanes].astype(F32) * soq[:, lanes].astype(F32)
        sgext[0:tokens, lanes] = (banded(mgext, toep_b, b) * gates).astype(BF16)

    @pl.when(me > 0)
    def _():
        push(SG_HALO, sgext.at[0:16, :], sgext.at[tokens : tokens + 16, :], {"seq": me - 1})

    def opened(packed, target):
        for p in range(slots // per_part):
            turned_rows = mm(swap[...], packed[p * part : (p + 1) * part, :]).astype(BF16)
            for b in range(blocks):
                target[p * per_part : (p + 1) * per_part, b * LANES : (b + 1) * LANES] = (
                    turned_rows[b * per_part : (b + 1) * per_part]
                )

    def closed(value, packed):
        for p in range(slots // per_part):
            piece = stacked(value[p * per_part : (p + 1) * per_part])
            packed[p * part : (p + 1) * part, :] = t_mm(swap[...], piece).astype(BF16)

    landed(X_OUT, xr)
    opened(xr, yx)
    codes_all[mine] = mm_t(down[0], yx[...])
    share(CODES, codes_all)

    @pl.when(me < n_seq - 1)
    def _():
        landed(SG_HALO, sgext.at[tokens : tokens + 16, :])

    @pl.when(me == n_seq - 1)
    def _():
        sgext[tokens : tokens + 16, :] = jnp.zeros((16, width), BF16)

    ahead = sgext[...].astype(F32)
    total = jnp.zeros((tokens, width), F32)
    for j in range(short_len):
        total = total + short_wide[j : j + 1, :] * ahead[j : j + tokens]
    delta_grad = (0.5 * total * sik[...].astype(F32)).astype(BF16)
    ds[...] = mm(place[...], stacked(delta_grad)).astype(BF16)
    split = 3 * n_seq // 8
    exchange(DG_OUT, ds, dr, first=split)

    def summed(ref):
        total = ref[0]
        for c in range(1, ref.shape[0]):
            total = total + ref[c]
        return total

    landed(CODES, codes_all.at[0 : n_ch - 1])
    codes = summed(codes_all).astype(BF16)
    closed((0.5 * t_mm(codes, up[0])).astype(BF16), us)
    exchange(DELTA_BACK, us, ur)
    exchange(DG_OUT, ds, dr, last=split)

    landed(DELTA_BACK, ur)
    delta = mm(place_t[...], ur[...]).astype(BF16).astype(F32)
    for b in range(blocks):
        lanes = slice(b * LANES, (b + 1) * LANES)
        siext[16 : 16 + tokens, lanes] = (
            sik[:, lanes].astype(F32)
            * (sfv[:, lanes].astype(F32) + delta[b * tokens : (b + 1) * tokens])
        ).astype(BF16)

    @pl.when(me < n_seq - 1)
    def _():
        push(SI_HALO, siext.at[tokens : tokens + 16, :], siext.at[0:16, :], {"seq": me + 1})

    @pl.when(me > 0)
    def _():
        landed(SI_HALO, siext.at[0:16, :])

    @pl.when(me == 0)
    def _():
        siext[0:16, :] = jnp.zeros((16, width), BF16)

    behind = siext[...].astype(F32)
    total = jnp.zeros((tokens, width), F32)
    for j in range(short_len):
        total = total + short_wide[j : j + 1, :] * behind[16 - j : 16 - j + tokens]
    medext[0:tokens, :] = (mik[...].astype(F32) * soq[...].astype(F32) * total).astype(BF16)

    @pl.when(me < n_seq - 1)
    def _():
        push(MED_HALO, medext.at[0:tokens, :], medext.at[tokens : 2 * tokens, :], {"seq": me + 1})

    landed(DG_OUT, dr)
    opened(dr, yd)
    cgrad_all[mine] = mm_t(up[0], yd[...])
    share(CODES_GRAD, cgrad_all)

    short_grad = sgext[0:tokens, :].astype(F32)
    fg[:, 8:16, :] = jnp.zeros((blocks, 8, LANES), F32)
    for j in range(short_len):
        line = jnp.sum(short_grad * behind[16 - j : 16 - j + tokens], axis=0, keepdims=True)
        for b in range(blocks):
            fg[b, 8 + j : 9 + j, :] = line[:, b * LANES : (b + 1) * LANES]

    @pl.when(me > 0)
    def _():
        landed(MED_HALO, medext.at[tokens : 2 * tokens, :])

    @pl.when(me == 0)
    def _():
        medext[tokens : 2 * tokens, :] = jnp.zeros((tokens, width), BF16)

    flip = jnp.where(row + col == tokens - 1, 1.0, 0.0).astype(BF16)

    @pl.loop(0, blocks)
    def _(b):
        lanes = lane_block(b)
        grads = mgext[0:tokens, lanes].astype(F32)
        data = jnp.concatenate(
            [
                mm(flip, medext[0:tokens, lanes]).astype(BF16),
                mm(flip, medext[tokens : 2 * tokens, lanes]).astype(BF16),
            ],
            axis=0,
        )
        for q in range(per_block):
            masked = jnp.where(lane_group == q, grads, 0.0).astype(BF16)
            product = mm_t(masked, data)
            merged = jnp.where(
                col + row >= tokens - 1, product[:, 0:tokens], product[:, tokens : 2 * tokens]
            )
            lined = pltpu.roll(merged, 1, 1, stride=1, stride_axis=0)
            fg[b, q : q + 1, :] = jnp.sum(lined, axis=0, keepdims=True)

    yr[my_y] = fg[my_y]

    @pl.loop(1, n_y)
    def _(step):
        peer = lax.rem(my_y + step, n_y)
        push(SUM_Y, fg.at[peer], yr.at[my_y], {"seq": my_z * n_y + peer})

    def respond(b):
        lanes = lane_block(b)
        response[:, lanes] = (
            banded(medext, toep_f, b) * moq[:, lanes].astype(F32)
        ).astype(BF16)

    landed(CODES_GRAD, cgrad_all.at[0 : n_ch - 1])
    codes_grad = summed(cgrad_all).astype(BF16)
    closed(t_mm(codes_grad, down[0]).astype(BF16), es)
    exchange(DX_BACK, es, er)

    @pl.loop(0, blocks // 2)
    def _(b):
        respond(b)

    landed(SUM_Y, yr.at[0 : n_y - 1])
    zr[my_z] = summed(yr)

    @pl.loop(1, n_z)
    def _(step):
        peer = lax.rem(my_z + step, n_z)
        push(SUM_Z, zr.at[my_z], zr.at[my_z], {"seq": peer * n_y + my_y})

    @pl.loop(blocks // 2, blocks)
    def _(b):
        respond(b)

    landed(SUM_Z, zr.at[0 : n_z - 1])
    fr[my_y] = summed(zr)

    @pl.loop(1, n_y)
    def _(step):
        peer = lax.rem(my_y + step, n_y)
        push(SPREAD_Y, fr.at[my_y], fr.at[my_y], {"seq": my_z * n_y + peer})

    weight_scale = 1.0 / math.sqrt(tokens)
    expander[0] = mm(codes, yd[...]) * weight_scale
    projector[0] = mm(codes_grad, yx[...]) * weight_scale

    landed(DX_BACK, er)
    back = mm(place_t[...], er[...]).astype(BF16)
    for b in range(blocks):
        dx_out[:, b * LANES : (b + 1) * LANES] = back[b * tokens : (b + 1) * tokens]

    @pl.when(me > 0)
    def _():
        gone(MG_HALO, mgext.at[0:tokens, :])
        gone(SG_HALO, sgext.at[0:16, :])

    @pl.when(me < n_seq - 1)
    def _():
        gone(SI_HALO, siext.at[tokens : tokens + 16, :])
        gone(MED_HALO, medext.at[0:tokens, :])

    for kind, ref in ((X_OUT, xs), (DG_OUT, ds), (DELTA_BACK, us), (DX_BACK, es)):
        gone(kind, ref.at[0 : (n_seq - 1) * chunk, :])
    gone(CODES, codes_all.at[0 : n_ch - 1])
    gone(CODES_GRAD, cgrad_all.at[0 : n_ch - 1])
    gone(SUM_Y, fg.at[0 : n_y - 1])
    gone(SUM_Z, zr.at[0 : n_z - 1])

    landed(SPREAD_Y, fr.at[0 : n_y - 1])
    gone(SPREAD_Y, fr.at[0 : n_y - 1])
    sums[...] = fr[...]


def finish(
    n_seq, response, dx, projector, expander, sums, rate,
    response_out, dx_out, projector_out, expander_out, brief, midrange,
):
    tokens, width = response.shape
    short_len, groups = brief.shape
    blocks, per_block, size = sums.shape[0], groups // sums.shape[0], width // groups
    response_out[...] = response[...]
    dx_out[...] = dx[...]
    projector_out[...] = projector[...]
    expander_out[...] = expander[...]
    eye = iota((groups, groups), 0) == iota((groups, groups), 1)
    rate_col = jnp.sum(jnp.where(eye, rate[...], 0.0), axis=1, keepdims=True)
    envelope = jnp.exp(-rate_col * iota((groups, LANES), 1).astype(F32))
    scale = 1.0 / math.sqrt(tokens * n_seq * size)
    for b in range(blocks):
        rows = slice(b * per_block, (b + 1) * per_block)
        midrange[rows, :] = sums[b, 0:8, :] * (envelope[rows] * scale)
    of_group = jnp.where(
        iota((groups, width), 1) // size == iota((groups, width), 0), 1.0, 0.0
    )
    lines = jnp.concatenate([sums[b, 8:16, :] for b in range(blocks)], axis=1)
    brief[...] = mm_t(lines, of_group, lax.Precision.HIGHEST)[0:short_len] * scale


def on_device(n_y, *arguments):
    x, down, storage = arguments[0], arguments[7], arguments[10]
    short_filter, medium_filter = arguments[11], arguments[12]
    tokens, width = x.shape
    n_seq, n_ch = lax.axis_size("seq"), lax.axis_size("ch")
    cap = max(2, 2 * tokens // n_seq)
    slots, blocks = n_seq * cap, width // LANES
    groups, breadth = short_filter.shape[0], down.shape[1]
    packed = pltpu.VMEM((slots * blocks, LANES), BF16)
    spread = pltpu.VMEM((slots, width), BF16)
    vmem = pl.BlockSpec(memory_space=pltpu.VMEM)
    arguments = list(arguments)
    arguments[9] = arguments[9].T
    arguments[10] = storage.reshape(1, n_seq)
    arguments[11] = short_filter.T
    arguments[13] = arguments[13].reshape(1, groups)
    outs = (
        jax.ShapeDtypeStruct((tokens, width), BF16),
        jax.ShapeDtypeStruct((tokens, width), BF16),
        jax.ShapeDtypeStruct((1, breadth, width), F32),
        jax.ShapeDtypeStruct((1, breadth, width), F32),
    )
    filters = (
        jax.ShapeDtypeStruct(short_filter.shape[::-1], F32),
        jax.ShapeDtypeStruct(medium_filter.shape, F32),
    )
    results = pl.pallas_call(
        functools.partial(kernel, n_seq, n_ch, n_y, cap),
        out_shape=outs + (jax.ShapeDtypeStruct((blocks, 16, LANES), F32),),
        in_specs=[vmem] * len(arguments),
        out_specs=[vmem] * (len(outs) + 1),
        scratch_shapes=[
            pltpu.VMEM((slots * blocks, width), BF16),
            pltpu.VMEM((width, slots * blocks), BF16),
            pltpu.VMEM((2 * LANES, 2 * LANES), BF16),
            pltpu.VMEM((groups, tokens, 2 * tokens), BF16),
            pltpu.VMEM((groups, tokens, 2 * tokens), BF16),
            pltpu.VMEM((2 * tokens, width), BF16),
            pltpu.VMEM((tokens + 16, width), BF16),
            pltpu.VMEM((tokens + 16, width), BF16),
            pltpu.VMEM((2 * tokens, width), BF16),
            packed, packed, packed, packed, packed, packed, packed, packed,
            spread, spread,
            pltpu.VMEM((n_ch, breadth, slots), F32),
            pltpu.VMEM((n_ch, breadth, slots), F32),
            pltpu.VMEM((blocks, 16, LANES), F32),
            pltpu.VMEM((n_y, 16, LANES), F32),
            pltpu.VMEM((n_seq // n_y, 16, LANES), F32),
            pltpu.VMEM((n_y, 16, LANES), F32),
            pltpu.VMEM((groups, LANES), F32),
            pltpu.VMEM((groups, LANES), F32),
            pltpu.SemaphoreType.DMA((13,)),
            pltpu.SemaphoreType.DMA((13,)),
        ],
        compiler_params=pltpu.CompilerParams(
            collective_id=0, has_side_effects=True, vmem_limit_bytes=56 * 1024 * 1024
        ),
    )(*arguments)
    *results, brief, midrange = pl.pallas_call(
        functools.partial(finish, n_seq),
        out_shape=outs + filters,
        in_specs=[vmem] * 6,
        out_specs=[vmem] * 6,
    )(*results, arguments[13])
    return (*results, brief.T, midrange)


def solution(mesh):
    tile, factor = P("seq", "ch"), P("seq", None, "ch")
    return jax.shard_map(
        functools.partial(on_device, 4),
        mesh=mesh,
        in_specs=(tile,) * 7
        + (factor, factor, P("seq", None), P(), P("ch", None), P("ch", None), P("ch")),
        out_specs=(tile, tile, factor, factor, P("ch", None), P("ch", None)),
        check_vma=False,
    )
```
